32 devices in a mesh: layer: 2 (over core), row: 4 (over y, x), col: 4 (over z).
Axes of the slice: x: 2, y: 2, z: 4, core: 2. Of those that a mesh axis runs over, the one named last changes fastest.
Arguments:
- lower_panels: bfloat16 [6, 5120, 2048], P('layer', 'row', 'col'), may hold values from -4 to 4
- upper_panels: bfloat16 [6, 5120, 2048], P('layer', 'col', 'row'), may hold values from -0.125 to 0.125
- lower_lists: int32 [2, 2], P('layer'), may hold values from 0 to 2
- upper_lists: int32 [2, 2], P('layer'), may hold values from 0 to 2
- block_counts: int32 [2], P('layer'), may hold values from 1 to 2, as said below
- ancestor: bfloat16 [2560, 2, 5120], P('row', 'layer', 'col'), may hold values from -6 to 6
- pivot_inverse: float32 [2560, 2], P('row', 'layer'), may hold values from 0.3 to 3
Outputs:
- updated: float32 [2560, 2, 5120], P('row', 'layer', 'col')
The draws below stay inside these ranges and needn't reach their ends.
Inputs may be any that keep to these rules, and one draw needn't show every extreme that they name: `block_counts`: each layer lists at least one pair; some layer lists exactly 2 and some layer exactly one. `lower_lists`: entries at slots from a layer's count onward are ignored. `upper_lists`: entries at slots from a layer's count onward are ignored.
All inputs are finite; a program needn't handle non-finite values.
Results may differ from the reference program's by a relative error of at most 0.0003.
Values may be sent and summed in bfloat16 or wider, within the bound.
No kernel may reach another device: no remote copies, remote signals or barrier semaphores. Data moves between devices by JAX's collectives and lax.ppermute only.
A program may use at most 128 MiB of HBM per device.

```python
import math
import jax
import jax.numpy as jnp
from jax import lax

ORDER = 5120
TILE = 2048
POOL = 3
LISTED = 2
LAYERS = 2
ROW_GROUPS = 2560


def draw_block_counts(key, part):
    values = jax.random.randint(key, (LAYERS,), 1, LISTED + 1).astype(jnp.int32)
    position = jax.random.randint(jax.random.fold_in(key, 7), (), 0, LAYERS).astype(jnp.int32)
    following = ((position + 1) % LAYERS).astype(jnp.int32)
    values = values.at[position].set(LISTED)
    values = values.at[following].set(1)
    return values.astype(jnp.int32)


def with_ends(result, own_key, least, largest):
    shape = result.shape
    place = [jax.random.randint(jax.random.fold_in(own_key, axis), (), 0, shape[axis]) for axis in range(len(shape))]
    result = result.at[tuple(place)].set(least)
    longest = shape.index(max(shape))
    place[longest] = (place[longest] + 1) % shape[longest]
    return result.at[tuple(place)].set(largest)


def levels(key, dims, split, low, largest):
    gain, own = 1.0, jax.random.fold_in(key, 6)
    for axis_at, parts in split:
        draws = jnp.exp(jax.random.uniform(jax.random.fold_in(own, axis_at), (parts,), jnp.float32, low / len(split), largest / len(split)))
        gain = gain * jnp.repeat(draws, dims[axis_at] // parts).reshape([-1 if axis == axis_at else 1 for axis in range(len(dims))])
    return gain


def normal_values(own_key, shape, spread, bound, split=(), kind=jnp.bfloat16):
    result = spread * jax.random.normal(own_key, shape, jnp.float32)
    if split:
        result = result * levels(own_key, shape, split, -0.22, 0.18)
    return jnp.clip(result, -bound, bound).astype(kind)


def setup_inputs(seed: int = 0) -> dict:
    splits = jax.random.split(jax.random.key(seed), 8)
    return {
        "lower_panels": normal_values(splits[0], (LAYERS * POOL, ORDER, TILE), 0.25, 4.0, ((0, 2), (1, 4), (2, 4))),
        "upper_panels": normal_values(splits[1], (LAYERS * POOL, ORDER, TILE), TILE ** -0.5, 0.125, ((0, 2), (1, 4), (2, 4))),
        "lower_lists": with_ends(jax.random.randint(splits[2], (LAYERS, LISTED), 0, POOL), jax.random.fold_in(splits[2], 1), 0, POOL - 1).astype(jnp.int32),
        "upper_lists": with_ends(jax.random.randint(splits[3], (LAYERS, LISTED), 0, POOL), jax.random.fold_in(splits[3], 1), 0, POOL - 1).astype(jnp.int32),
        "block_counts": draw_block_counts(jax.random.fold_in(splits[7], 71), 0),
        "ancestor": normal_values(splits[5], (ROW_GROUPS, LAYERS, ORDER), 1.0, 6.0, ((0, 4), (1, 2), (2, 4))),
        "pivot_inverse": jnp.clip(jnp.exp(math.log(3.0) - 2.3025851 * jax.random.uniform(splits[6], (ROW_GROUPS, LAYERS), jnp.float32) ** levels(splits[6], (ROW_GROUPS, LAYERS), ((0, 4), (1, 2)), -0.2, 0.2)), 0.3, 3.0),
    }


def reference(lower_panels, upper_panels, lower_lists, upper_lists, block_counts, ancestor, pivot_inverse):
    def layer_step(total, layer):
        for slot in range(LISTED):
            lower_index = (layer * POOL + lower_lists[layer, slot]).astype(jnp.int32)
            upper_index = (layer * POOL + upper_lists[layer, slot]).astype(jnp.int32)
            lower_one = lax.dynamic_index_in_dim(lower_panels, lower_index, 0, keepdims=False)
            upper_one = lax.dynamic_index_in_dim(upper_panels, upper_index, 0, keepdims=False)

            def add_pair(running):
                return running + jnp.dot(lower_one, upper_one.T, preferred_element_type=jnp.float32)

            def keep_same(running):
                return running

            total = lax.cond(slot < block_counts[layer], add_pair, keep_same, total)
        return total, None

    start_total = jnp.zeros((ORDER, ORDER), jnp.float32)
    total, ignored = lax.scan(layer_step, start_total, jnp.arange(LAYERS, dtype=jnp.int32))
    grouped = total.reshape(ROW_GROUPS, LAYERS, ORDER)
    return (ancestor.astype(jnp.float32) - grouped) * pivot_inverse[:, :, None]
```

```python
import functools

import jax
import jax.numpy as jnp
from jax import lax
from jax.experimental import pallas as pl
from jax.experimental.pallas import tpu as pltpu
from jax.sharding import PartitionSpec as P


PARTS = (4, 4, 4, 4)
TILE_N = 256
LANES = 128
MIB = 1024 * 1024
CHOOSE = 50


def general(
    lower_panels, upper_panels, lower_lists, upper_lists, block_counts, ancestor, pivot_inverse
):
    listed = lower_lists.shape[1]
    pairs_here = block_counts[0]
    rows_here = lower_panels.shape[1]
    cols_here = upper_panels.shape[1]
    layer_count = lax.axis_size("layer")
    groups_here = rows_here // layer_count
    slots = jnp.arange(listed, dtype=jnp.int32)
    live = slots < pairs_here
    lower_chosen = jnp.take(lower_panels, lower_lists[0], axis=0)
    lower_chosen = jnp.where(live[:, None, None], lower_chosen, jnp.zeros((), lower_chosen.dtype))
    upper_chosen = jnp.take(upper_panels, upper_lists[0], axis=0)
    upper_full = lax.all_gather(upper_chosen, "row", axis=2, tiled=True)
    lower_full = lax.all_gather(lower_chosen, "col", axis=2, tiled=True)
    inner_width = lower_full.shape[2]
    reordered = lower_full.reshape(listed, groups_here, layer_count, inner_width)
    reordered = jnp.transpose(reordered, (0, 2, 1, 3)).reshape(listed, rows_here, inner_width)
    mine = lax.psum_scatter(
        lax.dot_general(
            reordered, upper_full, (((0, 2), (0, 2)), ((), ())), preferred_element_type=jnp.float32
        ),
        "layer",
        scatter_dimension=0,
        tiled=True,
    )
    summed = mine.reshape(groups_here, 1, cols_here)
    return (ancestor.astype(jnp.float32) - summed) * pivot_inverse[:, :, None]


def split_rows(block, scratch, r):
    for g in range(scratch.shape[0]):
        scratch[g, r, :] = block[r, g * LANES : (g + 1) * LANES].astype(jnp.float32)


def every_second(scratch, start, out, kind):
    groups = [
        scratch[g, pl.ds(start, out, stride=2), :].astype(kind) for g in range(scratch.shape[0])
    ]
    return jnp.concatenate(groups, axis=1)


def fetch(panel, block, sems, tile):
    copies = []
    for i in range(block.shape[0] // tile):
        r = pl.ds(i * tile, tile)
        copies.append(pltpu.make_async_copy(panel.at[r, :], block.at[r, :], sems.at[i]))
        copies[-1].start()
    return copies


def head_kernel(lists, panels, lo, block, s0, sems):
    b = lax.axis_index("layer")
    tile = block.shape[0] // sems.shape[0]
    for i, copy in enumerate(fetch(panels.at[lists[0, 0]], block, sems, tile)):
        copy.wait()
        split_rows(block, s0, slice(i * tile, (i + 1) * tile))
        lo[i * tile // 2 : (i + 1) * tile // 2, :] = every_second(
            s0, i * tile + b, tile // 2, lo.dtype
        )


def lower_kernel(lists, panels, lk, ls, block0, block1, s0, s1, sems0, sems1):
    b = lax.axis_index("layer")
    half = block0.shape[1] // 2
    kind = lk.dtype
    tile = block0.shape[0] // sems0.shape[0]
    first_copies = fetch(panels.at[lists[0, 0]], block0, sems0, tile)
    second_copies = fetch(panels.at[lists[0, 1]], block1, sems1, tile)
    for i in range(len(first_copies)):
        first_copies[i].wait()
        r = slice(i * tile, (i + 1) * tile)
        split_rows(block0, s0, r)
        out = slice(i * tile // 2, (i + 1) * tile // 2)
        ls[out, : 2 * half] = every_second(s0, i * tile + 1 - b, tile // 2, kind)
    for i in range(len(second_copies)):
        second_copies[i].wait()
        r = slice(i * tile, (i + 1) * tile)
        split_rows(block1, s1, r)
        out = slice(i * tile // 2, (i + 1) * tile // 2)
        keep = every_second(s1, i * tile + b, tile // 2, kind)
        send = every_second(s1, i * tile + 1 - b, tile // 2, kind)

        @pl.when(b == 0)
        def _(out=out, keep=keep, send=send):
            lk[out, :] = keep
            ls[out, 2 * half : 3 * half] = send[:, half:]
            ls[out, 3 * half :] = send[:, :half]

        @pl.when(b != 0)
        def _(out=out, keep=keep, send=send):
            lk[out, :half] = keep[:, half:]
            lk[out, half:] = keep[:, :half]
            ls[out, 2 * half :] = send


def upper_kernel(lists, panels, uo, uk, us, sems0, sems1):
    b = lax.axis_index("layer")
    half = uk.shape[1]
    one = panels.at[lists[0, 1]]
    copies = [
        pltpu.make_async_copy(one.at[:, pl.ds((1 - b) * half, half)], us, sems1.at[0]),
        pltpu.make_async_copy(one.at[:, pl.ds(b * half, half)], uk, sems1.at[1]),
        pltpu.make_async_copy(panels.at[lists[0, 0]], uo, sems0.at[0]),
    ]
    for copy in copies:
        copy.start()
    for copy in copies:
        copy.wait()


def choose(kernel, lists, panels, shapes, blocks, scratch, tiles, limit):
    _, rows, inner = panels.shape
    vm = pl.BlockSpec(memory_space=pltpu.VMEM)
    moved = rows * inner * 2 * 2
    return pl.pallas_call(
        kernel,
        out_shape=tuple(jax.ShapeDtypeStruct(s, panels.dtype) for s in shapes),
        in_specs=[pl.BlockSpec(memory_space=pltpu.SMEM), pl.BlockSpec(memory_space=pl.ANY)],
        out_specs=(vm,) * len(shapes),
        scratch_shapes=[pltpu.VMEM((rows, inner), panels.dtype)] * blocks
        + [pltpu.VMEM((inner // LANES, rows, LANES), jnp.float32)] * scratch
        + [pltpu.SemaphoreType.DMA((n,)) for n in tiles],
        compiler_params=pltpu.CompilerParams(vmem_limit_bytes=limit * MIB),
        cost_estimate=pl.CostEstimate(flops=0, bytes_accessed=moved, transcendentals=0),
    )(lists, panels)


def lower_rest_kernel(sc, lk, lrecv, *outs):
    half = lk.shape[1] // 2
    start = 0
    for out in outs:
        r = pl.ds(start, out.shape[0])
        start += out.shape[0]
        out[:, half : 3 * half] = lrecv[r, : 2 * half]

        @pl.when(sc[0] == 2)
        def _(out=out, r=r):
            out[:, :half] = lk[r, :half]
            out[:, 3 * half :] = lk[r, half:]

        @pl.when(sc[0] != 2)
        def _(out=out, r=r):
            out[:, :half] = lrecv[r, 2 * half : 3 * half]
            out[:, 3 * half :] = lrecv[r, 3 * half :]


def upper_rest_kernel(sc, uo, uk, urecv, *outs):
    inner = uo.shape[1]
    rows = outs[0].shape[0]
    for i, out in enumerate(outs):
        r = pl.ds(i * rows, rows)
        out[:, :inner] = uo[r, :]

        @pl.when(sc[0] == 2)
        def _(out=out, r=r):
            out[:, inner:] = uk[r, :]

        @pl.when(sc[0] != 2)
        def _(out=out, r=r):
            out[:, inner:] = urecv[r, :]


def whole(kernel, out_shape, smem, *args):
    vm = pl.BlockSpec(memory_space=pltpu.VMEM)
    moved = sum(a.size * a.dtype.itemsize for a in args) * 2
    many = isinstance(out_shape, (list, tuple))
    return pl.pallas_call(
        kernel,
        out_shape=out_shape,
        in_specs=[pl.BlockSpec(memory_space=pltpu.SMEM)] + [vm] * len(args),
        out_specs=[vm] * len(out_shape) if many else vm,
        compiler_params=pltpu.CompilerParams(vmem_limit_bytes=16 * MIB),
        cost_estimate=pl.CostEstimate(flops=0, bytes_accessed=moved, transcendentals=0),
    )(smem, *args)


NT = (((1,), (1,)), ((), ()))


def first_kernel(parts, sc, *refs):
    per = 1 + parts
    own, m, n, q = (refs[i * per : (i + 1) * per] for i in range(4))
    ups = refs[4 * per : 4 * per + 16]
    acc, usel, lbuf, ubuf, lsem, usem, ssem = refs[4 * per + 16 :]
    inner = own[0].shape[1]
    width = ups[0].shape[1]
    urows = ups[0].shape[0]

    def start_u(slot, dst, sem):
        for j in range(4):

            @pl.when(slot == j)
            def _(j=j):
                for h in range(2):
                    r = pl.ds(h * urows, urows)
                    for side in range(2):
                        pltpu.make_async_copy(
                            ups[8 * side + 2 * j + h], dst.at[r, pl.ds(side * width, width)], sem
                        ).start()

    def start_l(pieces, dst, sem):
        pltpu.make_async_copy(pieces[0], dst.at[:, pl.ds(0, inner)], sem).start()
        at = 0
        for piece in pieces[1:]:
            pltpu.make_async_copy(
                piece, dst.at[pl.ds(at, piece.shape[0]), pl.ds(inner, 2 * inner)], sem
            ).start()
            at += piece.shape[0]

    def start(s):
        p = s % 2
        start_u(sc[s], ubuf.at[p], usem.at[p])
        if s == 0:
            start_l(own, lbuf.at[p], lsem.at[p])
        elif s == 1:
            start_l(m, lbuf.at[p], lsem.at[p])
        else:

            @pl.when(sc[4] != 0)
            def _():
                start_l(n, lbuf.at[p], lsem.at[p])

            @pl.when(sc[4] == 0)
            def _():
                start_l(q, lbuf.at[p], lsem.at[p])

    start(0)
    for s in range(3):
        p = s % 2
        if s < 2:
            start(s + 1)
        if s == 0:
            start_u(sc[3], usel, ssem)
        pltpu.make_async_copy(lbuf.at[p], lbuf.at[p], lsem.at[p]).wait()
        pltpu.make_async_copy(ubuf.at[p], ubuf.at[p], usem.at[p]).wait()

        for t in range(acc.shape[1] // TILE_N):
            cols = slice(t * TILE_N, (t + 1) * TILE_N)
            prod = lax.dot_general(
                lbuf[p], ubuf[p, cols, :], NT, preferred_element_type=jnp.float32
            )
            if s == 0:
                acc[:, cols] = prod
            else:
                acc[:, cols] += prod
    pltpu.make_async_copy(usel, usel, ssem).wait()


def first(sc, own, m, n, q, ups, groups, cols):
    parts = len(own) - 1
    bf = own[0].dtype
    inner = own[0].shape[1]
    width = 2 * ups[0].shape[1]
    anywhere = pl.BlockSpec(memory_space=pl.ANY)
    vm = pl.BlockSpec(memory_space=pltpu.VMEM)
    args = (*own, *m, *n, *q, *ups)
    return pl.pallas_call(
        functools.partial(first_kernel, parts),
        out_shape=(
            jax.ShapeDtypeStruct((groups, cols), jnp.float32),
            jax.ShapeDtypeStruct((cols, width), bf),
        ),
        in_specs=[pl.BlockSpec(memory_space=pltpu.SMEM)] + [anywhere] * len(args),
        out_specs=(vm, vm),
        scratch_shapes=[
            pltpu.VMEM((2, groups, 3 * inner), bf),
            pltpu.VMEM((2, cols, width), bf),
            pltpu.SemaphoreType.DMA((2,)),
            pltpu.SemaphoreType.DMA((2,)),
            pltpu.SemaphoreType.DMA,
        ],
        compiler_params=pltpu.CompilerParams(vmem_limit_bytes=60 * MIB),
        cost_estimate=pl.CostEstimate(
            flops=2 * groups * cols * width * 3,
            bytes_accessed=3 * (groups + cols) * width * 2,
            transcendentals=0,
        ),
        name="first",
    )(sc, *args)


def mid_kernel(sc, po, to, usel, acc, out):
    lo = jnp.where(sc[4] != 0, po[...], to[...])
    for t in range(acc.shape[1] // TILE_N):
        c = slice(t * TILE_N, (t + 1) * TILE_N)
        out[:, c] = acc[:, c] + lax.dot_general(
            lo, usel[c, : po.shape[1]], NT, preferred_element_type=jnp.float32
        )


def mid(sc, po, to, usel, acc):
    vm = pl.BlockSpec(memory_space=pltpu.VMEM)
    return pl.pallas_call(
        mid_kernel,
        out_shape=jax.ShapeDtypeStruct(acc.shape, acc.dtype),
        in_specs=[pl.BlockSpec(memory_space=pltpu.SMEM)] + [vm] * 4,
        out_specs=vm,
        input_output_aliases={4: 0},
        compiler_params=pltpu.CompilerParams(vmem_limit_bytes=20 * MIB),
        cost_estimate=pl.CostEstimate(
            flops=2 * acc.size * po.shape[1], bytes_accessed=acc.size * 8, transcendentals=0
        ),
        name="mid",
    )(sc, po, to, usel, acc)


def last_kernel(start, sc, pr, tr, usel, acc, anc, piv, *rest):
    out, buf, sem = rest[-3:]
    rows, width = pr.shape
    inner = usel.shape[1] - width
    lanes = piv.shape[1]
    r = slice(start, start + rows)
    lr = jnp.where(sc[4] != 0, pr[...], tr[...])
    cols = acc.shape[1]
    scale = piv[r, :]
    for t in range(cols // TILE_N):
        c = slice(t * TILE_N, (t + 1) * TILE_N)
        total = acc[r, c]
        total += lax.dot_general(lr, usel[c, inner:], NT, preferred_element_type=jnp.float32)
        ancf = anc[r, c].astype(jnp.float32)
        for h in range(TILE_N // lanes):
            k = slice(h * lanes, (h + 1) * lanes)
            buf[pl.ds(t * (TILE_N // lanes) + h, rows, stride=cols // lanes), :] = (
                ancf[:, k] - total[:, k]
            ) * scale
    size = buf.shape[0]
    copy = pltpu.make_async_copy(buf, out.at[pl.ds(start * cols // lanes, size), :], sem)
    copy.start()
    copy.wait()


def last(start, sc, pr, tr, usel, acc, anc, piv, before):
    groups, cols = acc.shape
    rows, width = pr.shape
    lanes = piv.shape[1]
    vm = pl.BlockSpec(memory_space=pltpu.VMEM)
    in_specs = [pl.BlockSpec(memory_space=pltpu.SMEM)] + [vm] * 6
    args = [sc, pr, tr, usel, acc, anc, piv]
    alias = {}
    if before is not None:
        in_specs.append(pl.BlockSpec(memory_space=pl.ANY))
        alias = {len(args): 0}
        args.append(before)
    return pl.pallas_call(
        functools.partial(last_kernel, start),
        out_shape=jax.ShapeDtypeStruct((groups * cols // lanes, lanes), jnp.float32),
        in_specs=in_specs,
        out_specs=pl.BlockSpec(memory_space=pl.ANY),
        scratch_shapes=[
            pltpu.VMEM((rows * cols // lanes, lanes), jnp.float32),
            pltpu.SemaphoreType.DMA,
        ],
        input_output_aliases=alias,
        compiler_params=pltpu.CompilerParams(vmem_limit_bytes=20 * MIB),
        cost_estimate=pl.CostEstimate(
            flops=2 * rows * cols * width,
            bytes_accessed=cols * width * 2 + rows * width * 4 + rows * cols * 10,
            transcendentals=0,
        ),
    )(*args)


def two_layers(
    lower_panels, upper_panels, lower_lists, upper_lists, block_counts, ancestor, pivot_inverse
):
    r = lax.axis_index("row").astype(jnp.int32)
    c = lax.axis_index("col").astype(jnp.int32)
    _, rows, inner = lower_panels.shape
    cols = upper_panels.shape[1]
    groups = rows // 2
    count = block_counts.astype(jnp.int32)
    swap = [(0, 1), (1, 0)]
    outer = [(0, 1), (1, 0), (2, 3), (3, 2)]
    middle = [(1, 2), (2, 1)]
    ends = [(1, 0), (2, 3)]
    across = [(0, 2), (2, 0), (1, 3), (3, 1)]

    (lo,) = choose(head_kernel, lower_lists, lower_panels, [(groups, inner)], 1, 1, (5,), 60)
    m0 = lax.ppermute(lo, "col", outer)
    n0 = lax.ppermute(lo, "col", middle)
    sizes = [(groups, inner), (groups, 2 * inner)]
    lk, ls = choose(lower_kernel, lower_lists, lower_panels, sizes, 2, 2, (5, 5), CHOOSE)
    lrecv = lax.ppermute(ls, "layer", swap)
    sizes = [(cols, inner), (cols, inner // 2), (cols, inner // 2)]
    uo, uk, us = choose(upper_kernel, upper_lists, upper_panels, sizes, 0, 0, (1, 2), CHOOSE)
    urecv = lax.ppermute(us, "layer", swap)
    bf = lo.dtype
    part = [
        jax.ShapeDtypeStruct((groups * share // sum(PARTS), 2 * inner), bf) for share in PARTS
    ]
    lr = whole(lower_rest_kernel, part, count, lk, lrecv)
    half = [jax.ShapeDtypeStruct((cols // 2, inner + inner // 2), bf)] * 2
    up = whole(upper_rest_kernel, half, count, uo, uk, urecv)
    own = [lo, *lr]
    m = [m0] + [lax.ppermute(x, "col", outer) for x in lr]
    n = [n0] + [lax.ppermute(x, "col", middle) for x in lr]
    xx = [lax.ppermute(x, "row", outer) for x in up]
    yy = [lax.ppermute(x, "row", across) for x in up]
    da = lax.ppermute(yy[0], "row", outer)
    db = lax.ppermute(xx[1], "row", across)
    mine = [*up, *xx, *yy, da, db]
    mate = [lax.ppermute(x, "layer", swap) for x in mine]
    p = [lax.ppermute(x, "col", middle) for x in m]
    q = [lax.ppermute(x, "col", ends) for x in n]
    t = [lax.ppermute(x, "col", ends) for x in p]

    low = c < 2
    inside = jnp.logical_and(c > 0, c < 3)
    sc = jnp.stack(
        [
            r ^ c,
            r ^ c ^ 1,
            r ^ jnp.where(low, 2, 1),
            r ^ jnp.where(low, 3, 0),
            inside.astype(jnp.int32),
        ]
    ).astype(jnp.int32)
    acc, usel = first(sc, own, m, n, q, [*mine, *mate], groups, cols)
    anc = ancestor.reshape(groups, cols)
    piv = jnp.broadcast_to(pivot_inverse, (groups, LANES))
    acc = mid(sc, p[0], t[0], usel, acc)
    out = None
    start = 0
    for x, y in zip(p[1:], t[1:]):
        out = last(start, sc, x, y, usel, acc, anc, piv, out)
        start += x.shape[0]
    return out.reshape(groups, 1, cols)


def per_device(*args):
    sizes = [lax.axis_size(a) for a in ("layer", "row", "col")]
    if sizes == [2, 4, 4]:
        return two_layers(*args)
    return general(*args)


def solution(mesh):
    in_specs = (
        P("layer", "row", "col"),
        P("layer", "col", "row"),
        P("layer", None),
        P("layer", None),
        P("layer"),
        P("row", "layer", "col"),
        P("row", "layer"),
    )
    out_specs = P("row", "layer", "col")
    return jax.shard_map(
        per_device, mesh=mesh, in_specs=in_specs, out_specs=out_specs, check_vma=False
    )
```

```python
import functools

import jax
import jax.numpy as jnp
from jax import lax
from jax.experimental import pallas as pl
from jax.experimental.pallas import tpu as pltpu
from jax.sharding import PartitionSpec as P


PIECES = ((0, 2, 0, 2), (2, 3, 0, 2), (3, 4, 0, 1), (3, 4, 1, 2))
TILE_N = 256
LANES = 128
MIB = 1024 * 1024
CHOOSE = 50


def general(
    lower_panels, upper_panels, lower_lists, upper_lists, block_counts, ancestor, pivot_inverse
):
    listed = lower_lists.shape[1]
    pairs_here = block_counts[0]
    rows_here = lower_panels.shape[1]
    cols_here = upper_panels.shape[1]
    layer_count = lax.axis_size("layer")
    groups_here = rows_here // layer_count
    slots = jnp.arange(listed, dtype=jnp.int32)
    live = slots < pairs_here
    lower_chosen = jnp.take(lower_panels, lower_lists[0], axis=0)
    lower_chosen = jnp.where(live[:, None, None], lower_chosen, jnp.zeros((), lower_chosen.dtype))
    upper_chosen = jnp.take(upper_panels, upper_lists[0], axis=0)
    upper_full = lax.all_gather(upper_chosen, "row", axis=2, tiled=True)
    lower_full = lax.all_gather(lower_chosen, "col", axis=2, tiled=True)
    inner_width = lower_full.shape[2]
    reordered = lower_full.reshape(listed, groups_here, layer_count, inner_width)
    reordered = jnp.transpose(reordered, (0, 2, 1, 3)).reshape(listed, rows_here, inner_width)
    mine = lax.psum_scatter(
        lax.dot_general(
            reordered, upper_full, (((0, 2), (0, 2)), ((), ())), preferred_element_type=jnp.float32
        ),
        "layer",
        scatter_dimension=0,
        tiled=True,
    )
    summed = mine.reshape(groups_here, 1, cols_here)
    return (ancestor.astype(jnp.float32) - summed) * pivot_inverse[:, :, None]


def split_rows(block, scratch, r):
    for g in range(scratch.shape[0]):
        scratch[g, r, :] = block[r, g * LANES : (g + 1) * LANES].astype(jnp.float32)


def every_second(scratch, start, out, kind):
    groups = [
        scratch[g, pl.ds(start, out, stride=2), :].astype(kind) for g in range(scratch.shape[0])
    ]
    return jnp.concatenate(groups, axis=1)


def fetch(panel, block, sems, tile):
    copies = []
    for i in range(block.shape[0] // tile):
        r = pl.ds(i * tile, tile)
        copies.append(pltpu.make_async_copy(panel.at[r, :], block.at[r, :], sems.at[i]))
        copies[-1].start()
    return copies


def head_kernel(lists, panels, lo, block, s0, sems):
    b = lax.axis_index("layer")
    tile = block.shape[0] // sems.shape[0]
    for i, copy in enumerate(fetch(panels.at[lists[0, 0]], block, sems, tile)):
        copy.wait()
        split_rows(block, s0, slice(i * tile, (i + 1) * tile))
        lo[i * tile // 2 : (i + 1) * tile // 2, :] = every_second(
            s0, i * tile + b, tile // 2, lo.dtype
        )


def lower_kernel(lists, panels, lk, ls, block0, block1, s0, s1, sems0, sems1):
    b = lax.axis_index("layer")
    half = block0.shape[1] // 2
    kind = lk.dtype
    tile = block0.shape[0] // sems0.shape[0]
    first_copies = fetch(panels.at[lists[0, 0]], block0, sems0, tile)
    second_copies = fetch(panels.at[lists[0, 1]], block1, sems1, tile)
    for i in range(len(first_copies)):
        first_copies[i].wait()
        r = slice(i * tile, (i + 1) * tile)
        split_rows(block0, s0, r)
        out = slice(i * tile // 2, (i + 1) * tile // 2)
        ls[out, : 2 * half] = every_second(s0, i * tile + 1 - b, tile // 2, kind)
    for i in range(len(second_copies)):
        second_copies[i].wait()
        r = slice(i * tile, (i + 1) * tile)
        split_rows(block1, s1, r)
        out = slice(i * tile // 2, (i + 1) * tile // 2)
        keep = every_second(s1, i * tile + b, tile // 2, kind)
        send = every_second(s1, i * tile + 1 - b, tile // 2, kind)

        @pl.when(b == 0)
        def _(out=out, keep=keep, send=send):
            lk[out, :] = keep
            ls[out, 2 * half : 3 * half] = send[:, half:]
            ls[out, 3 * half :] = send[:, :half]

        @pl.when(b != 0)
        def _(out=out, keep=keep, send=send):
            lk[out, :half] = keep[:, half:]
            lk[out, half:] = keep[:, :half]
            ls[out, 2 * half :] = send


def upper_kernel(lists, panels, uo, uk, us, sems0, sems1):
    b = lax.axis_index("layer")
    half = uk.shape[1]
    one = panels.at[lists[0, 1]]
    copies = [
        pltpu.make_async_copy(one.at[:, pl.ds((1 - b) * half, half)], us, sems1.at[0]),
        pltpu.make_async_copy(one.at[:, pl.ds(b * half, half)], uk, sems1.at[1]),
        pltpu.make_async_copy(panels.at[lists[0, 0]], uo, sems0.at[0]),
    ]
    for copy in copies:
        copy.start()
    for copy in copies:
        copy.wait()


def choose(kernel, lists, panels, shapes, blocks, scratch, tiles, limit):
    _, rows, inner = panels.shape
    vm = pl.BlockSpec(memory_space=pltpu.VMEM)
    moved = rows * inner * 2 * 2
    return pl.pallas_call(
        kernel,
        out_shape=tuple(jax.ShapeDtypeStruct(s, panels.dtype) for s in shapes),
        in_specs=[pl.BlockSpec(memory_space=pltpu.SMEM), pl.BlockSpec(memory_space=pl.ANY)],
        out_specs=(vm,) * len(shapes),
        scratch_shapes=[pltpu.VMEM((rows, inner), panels.dtype)] * blocks
        + [pltpu.VMEM((inner // LANES, rows, LANES), jnp.float32)] * scratch
        + [pltpu.SemaphoreType.DMA((n,)) for n in tiles],
        compiler_params=pltpu.CompilerParams(vmem_limit_bytes=limit * MIB),
        cost_estimate=pl.CostEstimate(flops=0, bytes_accessed=moved, transcendentals=0),
    )(lists, panels)


def lower_rest_kernel(sc, lk, lrecv, *outs):
    half = lk.shape[1] // 2
    quarter = lk.shape[0] // 4
    two = sc[0] == 2

    for (r0, r1, c0, c1), out in zip(PIECES, outs):
        r = pl.ds(r0 * quarter, (r1 - r0) * quarter)
        base = 2 * half * c0
        for at in range(base, 2 * half * c1, half):
            to = pl.ds(at - base, half)
            k = at // half
            if k in (1, 2):
                out[:, to] = lrecv[r, pl.ds(at - half, half)]
                continue
            part = pl.ds(0 if k == 0 else half, half)
            other = pl.ds(2 * half if k == 0 else 3 * half, half)

            @pl.when(two)
            def _(out=out, r=r, to=to, part=part):
                out[:, to] = lk[r, part]

            @pl.when(jnp.logical_not(two))
            def _(out=out, r=r, to=to, other=other):
                out[:, to] = lrecv[r, other]


def upper_rest_kernel(sc, uo, uk, urecv, *outs):
    inner = uo.shape[1]
    rows = outs[0].shape[0]
    for i, out in enumerate(outs):
        r = pl.ds(i * rows, rows)
        out[:, :inner] = uo[r, :]

        @pl.when(sc[0] == 2)
        def _(out=out, r=r):
            out[:, inner:] = uk[r, :]

        @pl.when(sc[0] != 2)
        def _(out=out, r=r):
            out[:, inner:] = urecv[r, :]


def whole(kernel, out_shape, smem, *args):
    vm = pl.BlockSpec(memory_space=pltpu.VMEM)
    moved = sum(a.size * a.dtype.itemsize for a in args) * 2
    many = isinstance(out_shape, (list, tuple))
    return pl.pallas_call(
        kernel,
        out_shape=out_shape,
        in_specs=[pl.BlockSpec(memory_space=pltpu.SMEM)] + [vm] * len(args),
        out_specs=[vm] * len(out_shape) if many else vm,
        compiler_params=pltpu.CompilerParams(vmem_limit_bytes=16 * MIB),
        cost_estimate=pl.CostEstimate(flops=0, bytes_accessed=moved, transcendentals=0),
    )(smem, *args)


NT = (((1,), (1,)), ((), ()))


def first_kernel(parts, sc, *refs):
    per = 1 + parts
    own, m, n, q = (refs[i * per : (i + 1) * per] for i in range(4))
    ups = refs[4 * per : 4 * per + 16]
    acc, usel, lbuf, ubuf, lsem, usem, ssem = refs[4 * per + 16 :]
    inner = own[0].shape[1]
    width = ups[0].shape[1]
    urows = ups[0].shape[0]

    def start_u(slot, dst, sem):
        for j in range(4):

            @pl.when(slot == j)
            def _(j=j):
                for h in range(2):
                    r = pl.ds(h * urows, urows)
                    for side in range(2):
                        pltpu.make_async_copy(
                            ups[8 * side + 2 * j + h], dst.at[r, pl.ds(side * width, width)], sem
                        ).start()

    def start_l(pieces, dst, sem):
        pltpu.make_async_copy(pieces[0], dst.at[:, pl.ds(0, inner)], sem).start()
        quarter = dst.shape[0] // 4
        for (r0, r1, c0, c1), piece in zip(PIECES, pieces[1:]):
            r = pl.ds(r0 * quarter, (r1 - r0) * quarter)
            pltpu.make_async_copy(
                piece, dst.at[r, pl.ds((1 + c0) * inner, (c1 - c0) * inner)], sem
            ).start()

    def start(s):
        p = s % 2
        start_u(sc[s], ubuf.at[p], usem.at[p])
        if s == 0:
            start_l(own, lbuf.at[p], lsem.at[p])
        elif s == 1:
            start_l(m, lbuf.at[p], lsem.at[p])
        else:

            @pl.when(sc[4] != 0)
            def _():
                start_l(n, lbuf.at[p], lsem.at[p])

            @pl.when(sc[4] == 0)
            def _():
                start_l(q, lbuf.at[p], lsem.at[p])

    start(0)
    for s in range(3):
        p = s % 2
        if s < 2:
            start(s + 1)
        if s == 0:
            start_u(sc[3], usel, ssem)
        pltpu.make_async_copy(lbuf.at[p], lbuf.at[p], lsem.at[p]).wait()
        pltpu.make_async_copy(ubuf.at[p], ubuf.at[p], usem.at[p]).wait()

        for t in range(acc.shape[1] // TILE_N):
            cols = slice(t * TILE_N, (t + 1) * TILE_N)
            prod = lax.dot_general(
                lbuf[p], ubuf[p, cols, :], NT, preferred_element_type=jnp.float32
            )
            if s == 0:
                acc[:, cols] = prod
            else:
                acc[:, cols] += prod
    pltpu.make_async_copy(usel, usel, ssem).wait()


def first(sc, own, m, n, q, ups, groups, cols):
    parts = len(own) - 1
    bf = own[0].dtype
    inner = own[0].shape[1]
    width = 2 * ups[0].shape[1]
    anywhere = pl.BlockSpec(memory_space=pl.ANY)
    vm = pl.BlockSpec(memory_space=pltpu.VMEM)
    args = (*own, *m, *n, *q, *ups)
    return pl.pallas_call(
        functools.partial(first_kernel, parts),
        out_shape=(
            jax.ShapeDtypeStruct((groups, cols), jnp.float32),
            jax.ShapeDtypeStruct((cols, width), bf),
        ),
        in_specs=[pl.BlockSpec(memory_space=pltpu.SMEM)] + [anywhere] * len(args),
        out_specs=(vm, vm),
        scratch_shapes=[
            pltpu.VMEM((2, groups, 3 * inner), bf),
            pltpu.VMEM((2, cols, width), bf),
            pltpu.SemaphoreType.DMA((2,)),
            pltpu.SemaphoreType.DMA((2,)),
            pltpu.SemaphoreType.DMA,
        ],
        compiler_params=pltpu.CompilerParams(vmem_limit_bytes=60 * MIB),
        cost_estimate=pl.CostEstimate(
            flops=2 * groups * cols * width * 3,
            bytes_accessed=3 * (groups + cols) * width * 2,
            transcendentals=0,
        ),
        name="first",
    )(sc, *args)


def latest(p, t):
    c = lax.axis_index("col")
    inside = jnp.logical_and(c > 0, c < lax.axis_size("col") - 1)
    return jnp.where(inside, p[...], t[...])


def mid_kernel(start, at, p, t, usel, acc, out):
    rows, width = out.shape[0], p.shape[1]
    lower = latest(p, t)
    for i in range(acc.shape[1] // TILE_N):
        c = slice(i * TILE_N, (i + 1) * TILE_N)
        out[:, c] = acc[start : start + rows, c] + lax.dot_general(
            lower, usel[c, at : at + width], NT, preferred_element_type=jnp.float32
        )


def mid(start, at, p, t, usel, acc):
    rows, width = p.shape
    cols = acc.shape[1]
    vm = pl.BlockSpec(memory_space=pltpu.VMEM)
    return pl.pallas_call(
        functools.partial(mid_kernel, start, at),
        out_shape=jax.ShapeDtypeStruct((rows, cols), acc.dtype),
        in_specs=[vm] * 4,
        out_specs=vm,
        compiler_params=pltpu.CompilerParams(vmem_limit_bytes=20 * MIB),
        cost_estimate=pl.CostEstimate(
            flops=2 * rows * cols * width, bytes_accessed=rows * cols * 8, transcendentals=0
        ),
    )(p, t, usel, acc)


def stage_kernel(x, acc, out):
    out[...] = x[...]


def stage(x, acc):
    vm = pl.BlockSpec(memory_space=pltpu.VMEM)
    return pl.pallas_call(
        stage_kernel,
        out_shape=jax.ShapeDtypeStruct(x.shape, x.dtype),
        in_specs=[vm, pl.BlockSpec(memory_space=pl.ANY)],
        out_specs=vm,
        compiler_params=pltpu.CompilerParams(vmem_limit_bytes=20 * MIB),
        cost_estimate=pl.CostEstimate(flops=0, bytes_accessed=4 * x.size, transcendentals=0),
        name="stage",
    )(x, acc)


def last_kernel(start, within, at, p, t, usel, acc, anc, piv, *rest):
    out, total, buf, sems = rest[-4:]
    rows, width = p.shape
    lanes = piv.shape[1]
    lower = latest(p, t)
    cols = acc.shape[1]
    per = cols // lanes
    for i in range(cols // TILE_N):
        c = slice(i * TILE_N, (i + 1) * TILE_N)
        total[:, c] = acc[within : within + rows, c] + lax.dot_general(
            lower, usel[c, at : at + width], NT, preferred_element_type=jnp.float32
        )
    some = rows // sems.shape[0]
    copies = []
    for g in range(sems.shape[0]):
        r = slice(g * some, (g + 1) * some)
        full = slice(start + g * some, start + (g + 1) * some)
        scale = piv[full, :]
        for h in range(per):
            k = slice(h * lanes, (h + 1) * lanes)
            buf[pl.ds(g * some * per + h, some, stride=per), :] = (
                anc[full, k].astype(jnp.float32) - total[r, k]
            ) * scale
        size = some * per
        copies.append(
            pltpu.make_async_copy(
                buf.at[pl.ds(g * size, size), :],
                out.at[pl.ds(start * per + g * size, size), :],
                sems.at[g],
            )
        )
        copies[-1].start()
    for copy in copies:
        copy.wait()


def last(start, within, at, p, t, usel, acc, anc, piv, before):
    groups, cols = anc.shape
    rows, width = p.shape
    lanes = piv.shape[1]
    vm = pl.BlockSpec(memory_space=pltpu.VMEM)
    in_specs = [vm] * 6
    args = [p, t, usel, acc, anc, piv]
    alias = {}
    if before is not None:
        in_specs.append(pl.BlockSpec(memory_space=pl.ANY))
        alias = {len(args): 0}
        args.append(before)
    return pl.pallas_call(
        functools.partial(last_kernel, start, within, at),
        out_shape=jax.ShapeDtypeStruct((groups * cols // lanes, lanes), jnp.float32),
        in_specs=in_specs,
        out_specs=pl.BlockSpec(memory_space=pl.ANY),
        scratch_shapes=[
            pltpu.VMEM((rows, cols), jnp.float32),
            pltpu.VMEM((rows * cols // lanes, lanes), jnp.float32),
            pltpu.SemaphoreType.DMA((2,)),
        ],
        input_output_aliases=alias,
        compiler_params=pltpu.CompilerParams(vmem_limit_bytes=20 * MIB),
        cost_estimate=pl.CostEstimate(
            flops=2 * rows * cols * width,
            bytes_accessed=cols * width * 2 + rows * width * 4 + rows * cols * 10,
            transcendentals=0,
        ),
    )(*args)


def two_layers(
    lower_panels, upper_panels, lower_lists, upper_lists, block_counts, ancestor, pivot_inverse
):
    r = lax.axis_index("row").astype(jnp.int32)
    c = lax.axis_index("col").astype(jnp.int32)
    _, rows, inner = lower_panels.shape
    cols = upper_panels.shape[1]
    groups = rows // 2
    count = block_counts.astype(jnp.int32)
    swap = [(0, 1), (1, 0)]
    outer = [(0, 1), (1, 0), (2, 3), (3, 2)]
    middle = [(1, 2), (2, 1)]
    ends = [(1, 0), (2, 3)]
    across = [(0, 2), (2, 0), (1, 3), (3, 1)]

    (lo,) = choose(head_kernel, lower_lists, lower_panels, [(groups, inner)], 1, 1, (5,), CHOOSE)
    m0 = lax.ppermute(lo, "col", outer)
    n0 = lax.ppermute(lo, "col", middle)
    sizes = [(groups, inner), (groups, 2 * inner)]
    lk, ls = choose(lower_kernel, lower_lists, lower_panels, sizes, 2, 2, (5, 5), CHOOSE)
    lrecv = lax.ppermute(ls, "layer", swap)
    sizes = [(cols, inner), (cols, inner // 2), (cols, inner // 2)]
    uo, uk, us = choose(upper_kernel, upper_lists, upper_panels, sizes, 0, 0, (1, 2), CHOOSE)
    urecv = lax.ppermute(us, "layer", swap)
    bf = lo.dtype
    quarter = groups // 4
    part = [
        jax.ShapeDtypeStruct(((r1 - r0) * quarter, (c1 - c0) * inner), bf)
        for r0, r1, c0, c1 in PIECES
    ]
    lr = whole(lower_rest_kernel, part, count, lk, lrecv)
    half = [jax.ShapeDtypeStruct((cols // 2, inner + inner // 2), bf)] * 2
    up = whole(upper_rest_kernel, half, count, uo, uk, urecv)
    own = [lo, *lr]
    m = [m0] + [lax.ppermute(x, "col", outer) for x in lr]
    n = [n0] + [lax.ppermute(x, "col", middle) for x in lr]
    xx = [lax.ppermute(x, "row", outer) for x in up]
    yy = [lax.ppermute(x, "row", across) for x in up]
    da = lax.ppermute(yy[0], "row", outer)
    db = lax.ppermute(xx[1], "row", across)
    mine = [*up, *xx, *yy, da, db]
    mate = [lax.ppermute(x, "layer", swap) for x in mine]
    p = [lax.ppermute(x, "col", middle) for x in m]
    q = [lax.ppermute(x, "col", ends) for x in n]
    t = [lax.ppermute(x, "col", ends) for x in p]

    low = c < 2
    inside = jnp.logical_and(c > 0, c < 3)
    sc = jnp.stack(
        [
            r ^ c,
            r ^ c ^ 1,
            r ^ jnp.where(low, 2, 1),
            r ^ jnp.where(low, 3, 0),
            inside.astype(jnp.int32),
        ]
    ).astype(jnp.int32)
    acc, usel = first(sc, own, m, n, q, [*mine, *mate], groups, cols)
    anc = ancestor.reshape(groups, cols)
    piv = jnp.broadcast_to(pivot_inverse, (groups, LANES))
    acc = mid(0, 0, p[0], t[0], usel, acc)
    p[-1] = stage(p[-1], acc)
    out = None
    for (r0, _, c0, c1), x, y in zip(PIECES, p[1:], t[1:]):
        start, within, at = r0 * quarter, r0 * quarter, (1 + c0) * inner
        if c1 == 1:
            tail = mid(start, at, x, y, usel, acc)
            continue
        if c0 == 1:
            acc, within = tail, 0
        out = last(start, within, at, x, y, usel, acc, anc, piv, out)
    return out.reshape(groups, 1, cols)


def per_device(*args):
    sizes = [lax.axis_size(a) for a in ("layer", "row", "col")]
    if sizes == [2, 4, 4]:
        return two_layers(*args)
    return general(*args)


def solution(mesh):
    in_specs = (
        P("layer", "row", "col"),
        P("layer", "col", "row"),
        P("layer", None),
        P("layer", None),
        P("layer"),
        P("row", "layer", "col"),
        P("row", "layer"),
    )
    out_specs = P("row", "layer", "col")
    return jax.shard_map(
        per_device, mesh=mesh, in_specs=in_specs, out_specs=out_specs, check_vma=False
    )
```

```python
import functools

import jax
import jax.numpy as jnp
from jax import lax
from jax.experimental import pallas as pl
from jax.experimental.pallas import tpu as pltpu
from jax.sharding import PartitionSpec as P


PIECES = ((0, 2, 0, 2), (2, 3, 0, 2), (3, 4, 0, 1), (3, 4, 1, 2))
TILE_N = 256
LANES = 128
MIB = 1024 * 1024
CHOOSE = 50


def general(
    lower_panels, upper_panels, lower_lists, upper_lists, block_counts, ancestor, pivot_inverse
):
    listed = lower_lists.shape[1]
    pairs_here = block_counts[0]
    rows_here = lower_panels.shape[1]
    cols_here = upper_panels.shape[1]
    layer_count = lax.axis_size("layer")
    groups_here = rows_here // layer_count
    slots = jnp.arange(listed, dtype=jnp.int32)
    live = slots < pairs_here
    lower_chosen = jnp.take(lower_panels, lower_lists[0], axis=0)
    lower_chosen = jnp.where(live[:, None, None], lower_chosen, jnp.zeros((), lower_chosen.dtype))
    upper_chosen = jnp.take(upper_panels, upper_lists[0], axis=0)
    upper_full = lax.all_gather(upper_chosen, "row", axis=2, tiled=True)
    lower_full = lax.all_gather(lower_chosen, "col", axis=2, tiled=True)
    inner_width = lower_full.shape[2]
    reordered = lower_full.reshape(listed, groups_here, layer_count, inner_width)
    reordered = jnp.transpose(reordered, (0, 2, 1, 3)).reshape(listed, rows_here, inner_width)
    mine = lax.psum_scatter(
        lax.dot_general(
            reordered, upper_full, (((0, 2), (0, 2)), ((), ())), preferred_element_type=jnp.float32
        ),
        "layer",
        scatter_dimension=0,
        tiled=True,
    )
    summed = mine.reshape(groups_here, 1, cols_here)
    return (ancestor.astype(jnp.float32) - summed) * pivot_inverse[:, :, None]


def split_rows(block, scratch, r):
    for g in range(scratch.shape[0]):
        scratch[g, r, :] = block[r, g * LANES : (g + 1) * LANES].astype(jnp.float32)


def every_second(scratch, start, out, kind):
    groups = [
        scratch[g, pl.ds(start, out, stride=2), :].astype(kind) for g in range(scratch.shape[0])
    ]
    return jnp.concatenate(groups, axis=1)


def fetch(panel, block, sems, tile):
    copies = []
    for i in range(block.shape[0] // tile):
        r = pl.ds(i * tile, tile)
        copies.append(pltpu.make_async_copy(panel.at[r, :], block.at[r, :], sems.at[i]))
        copies[-1].start()
    return copies


def head_kernel(lists, panels, lo, block, s0, sems):
    b = lax.axis_index("layer")
    tile = block.shape[0] // sems.shape[0]
    row = lists[...]
    first_slot = lax.broadcasted_iota(jnp.int32, row.shape, 1) == 0
    chosen = jnp.sum(jnp.where(first_slot, row, 0))
    for i, copy in enumerate(fetch(panels.at[chosen], block, sems, tile)):
        copy.wait()
        split_rows(block, s0, slice(i * tile, (i + 1) * tile))
        lo[i * tile // 2 : (i + 1) * tile // 2, :] = every_second(
            s0, i * tile + b, tile // 2, lo.dtype
        )


def lower_kernel(lists, panels, lk, ls, block0, block1, s0, s1, sems0, sems1):
    b = lax.axis_index("layer")
    half = block0.shape[1] // 2
    kind = lk.dtype
    tile = block0.shape[0] // sems0.shape[0]
    first_copies = fetch(panels.at[lists[0, 0]], block0, sems0, tile)
    second_copies = fetch(panels.at[lists[0, 1]], block1, sems1, tile)
    for i in range(len(first_copies)):
        first_copies[i].wait()
        r = slice(i * tile, (i + 1) * tile)
        split_rows(block0, s0, r)
        out = slice(i * tile // 2, (i + 1) * tile // 2)
        ls[out, : 2 * half] = every_second(s0, i * tile + 1 - b, tile // 2, kind)
    for i in range(len(second_copies)):
        second_copies[i].wait()
        r = slice(i * tile, (i + 1) * tile)
        split_rows(block1, s1, r)
        out = slice(i * tile // 2, (i + 1) * tile // 2)
        keep = every_second(s1, i * tile + b, tile // 2, kind)
        send = every_second(s1, i * tile + 1 - b, tile // 2, kind)

        @pl.when(b == 0)
        def _(out=out, keep=keep, send=send):
            lk[out, :] = keep
            ls[out, 2 * half : 3 * half] = send[:, half:]
            ls[out, 3 * half :] = send[:, :half]

        @pl.when(b != 0)
        def _(out=out, keep=keep, send=send):
            lk[out, :half] = keep[:, half:]
            lk[out, half:] = keep[:, :half]
            ls[out, 2 * half :] = send


def upper_kernel(lists, panels, uo, uk, us, sems0, sems1):
    b = lax.axis_index("layer")
    half = uk.shape[1]
    one = panels.at[lists[0, 1]]
    copies = [
        pltpu.make_async_copy(one.at[:, pl.ds((1 - b) * half, half)], us, sems1.at[0]),
        pltpu.make_async_copy(one.at[:, pl.ds(b * half, half)], uk, sems1.at[1]),
        pltpu.make_async_copy(panels.at[lists[0, 0]], uo, sems0.at[0]),
    ]
    for copy in copies:
        copy.start()
    for copy in copies:
        copy.wait()


def choose(kernel, lists, panels, shapes, blocks, scratch, tiles, near=pltpu.SMEM):
    _, rows, inner = panels.shape
    vm = pl.BlockSpec(memory_space=pltpu.VMEM)
    moved = rows * inner * 2 * 2
    return pl.pallas_call(
        kernel,
        out_shape=tuple(jax.ShapeDtypeStruct(s, panels.dtype) for s in shapes),
        in_specs=[pl.BlockSpec(memory_space=near), pl.BlockSpec(memory_space=pl.ANY)],
        out_specs=(vm,) * len(shapes),
        scratch_shapes=[pltpu.VMEM((rows, inner), panels.dtype)] * blocks
        + [pltpu.VMEM((inner // LANES, rows, LANES), jnp.float32)] * scratch
        + [pltpu.SemaphoreType.DMA((n,)) for n in tiles],
        compiler_params=pltpu.CompilerParams(vmem_limit_bytes=CHOOSE * MIB),
        cost_estimate=pl.CostEstimate(flops=0, bytes_accessed=moved, transcendentals=0),
    )(lists, panels)


def lower_rest_kernel(sc, lk, lrecv, *outs):
    half = lk.shape[1] // 2
    quarter = lk.shape[0] // 4
    two = sc[0] == 2

    for (r0, r1, c0, c1), out in zip(PIECES, outs):
        r = pl.ds(r0 * quarter, (r1 - r0) * quarter)
        base = 2 * half * c0
        for at in range(base, 2 * half * c1, half):
            to = pl.ds(at - base, half)
            k = at // half
            if k in (1, 2):
                out[:, to] = lrecv[r, pl.ds(at - half, half)]
                continue
            part = pl.ds(0 if k == 0 else half, half)
            other = pl.ds(2 * half if k == 0 else 3 * half, half)

            @pl.when(two)
            def _(out=out, r=r, to=to, part=part):
                out[:, to] = lk[r, part]

            @pl.when(jnp.logical_not(two))
            def _(out=out, r=r, to=to, other=other):
                out[:, to] = lrecv[r, other]


def upper_rest_kernel(sc, uo, uk, urecv, *outs):
    inner = uo.shape[1]
    rows = outs[0].shape[0]
    for i, out in enumerate(outs):
        r = pl.ds(i * rows, rows)
        out[:, :inner] = uo[r, :]

        @pl.when(sc[0] == 2)
        def _(out=out, r=r):
            out[:, inner:] = uk[r, :]

        @pl.when(sc[0] != 2)
        def _(out=out, r=r):
            out[:, inner:] = urecv[r, :]


def whole(kernel, out_shape, smem, *args):
    vm = pl.BlockSpec(memory_space=pltpu.VMEM)
    moved = sum(a.size * a.dtype.itemsize for a in args) * 2
    many = isinstance(out_shape, (list, tuple))
    return pl.pallas_call(
        kernel,
        out_shape=out_shape,
        in_specs=[pl.BlockSpec(memory_space=pltpu.SMEM)] + [vm] * len(args),
        out_specs=[vm] * len(out_shape) if many else vm,
        compiler_params=pltpu.CompilerParams(vmem_limit_bytes=16 * MIB),
        cost_estimate=pl.CostEstimate(flops=0, bytes_accessed=moved, transcendentals=0),
    )(smem, *args)


NT = (((1,), (1,)), ((), ()))


def first_kernel(parts, sc, *refs):
    per = 1 + parts
    own, m, n, q = (refs[i * per : (i + 1) * per] for i in range(4))
    ups = refs[4 * per : 4 * per + 16]
    acc, usel, lbuf, ubuf, lsem, usem, ssem = refs[4 * per + 16 :]
    inner = own[0].shape[1]
    width = ups[0].shape[1]
    urows = ups[0].shape[0]

    def start_u(slot, dst, sem):
        for j in range(4):

            @pl.when(slot == j)
            def _(j=j):
                for h in range(2):
                    r = pl.ds(h * urows, urows)
                    for side in range(2):
                        pltpu.make_async_copy(
                            ups[8 * side + 2 * j + h], dst.at[r, pl.ds(side * width, width)], sem
                        ).start()

    def start_l(pieces, dst, sem):
        pltpu.make_async_copy(pieces[0], dst.at[:, pl.ds(0, inner)], sem).start()
        quarter = dst.shape[0] // 4
        for (r0, r1, c0, c1), piece in zip(PIECES, pieces[1:]):
            r = pl.ds(r0 * quarter, (r1 - r0) * quarter)
            pltpu.make_async_copy(
                piece, dst.at[r, pl.ds((1 + c0) * inner, (c1 - c0) * inner)], sem
            ).start()

    def start(s):
        p = s % 2
        start_u(sc[s], ubuf.at[p], usem.at[p])
        if s == 0:
            start_l(own, lbuf.at[p], lsem.at[p])
        elif s == 1:
            start_l(m, lbuf.at[p], lsem.at[p])
        else:

            @pl.when(sc[4] != 0)
            def _():
                start_l(n, lbuf.at[p], lsem.at[p])

            @pl.when(sc[4] == 0)
            def _():
                start_l(q, lbuf.at[p], lsem.at[p])

    start(0)
    for s in range(3):
        p = s % 2
        if s < 2:
            start(s + 1)
        if s == 0:
            start_u(sc[3], usel, ssem)
        pltpu.make_async_copy(lbuf.at[p], lbuf.at[p], lsem.at[p]).wait()
        pltpu.make_async_copy(ubuf.at[p], ubuf.at[p], usem.at[p]).wait()

        for t in range(acc.shape[1] // TILE_N):
            cols = slice(t * TILE_N, (t + 1) * TILE_N)
            prod = lax.dot_general(
                lbuf[p], ubuf[p, cols, :], NT, preferred_element_type=jnp.float32
            )
            if s == 0:
                acc[:, cols] = prod
            else:
                acc[:, cols] += prod
    pltpu.make_async_copy(usel, usel, ssem).wait()


def first(sc, own, m, n, q, ups, groups, cols):
    parts = len(own) - 1
    bf = own[0].dtype
    inner = own[0].shape[1]
    width = 2 * ups[0].shape[1]
    anywhere = pl.BlockSpec(memory_space=pl.ANY)
    vm = pl.BlockSpec(memory_space=pltpu.VMEM)
    args = (*own, *m, *n, *q, *ups)
    return pl.pallas_call(
        functools.partial(first_kernel, parts),
        out_shape=(
            jax.ShapeDtypeStruct((groups, cols), jnp.float32),
            jax.ShapeDtypeStruct((cols, width), bf),
        ),
        in_specs=[pl.BlockSpec(memory_space=pltpu.SMEM)] + [anywhere] * len(args),
        out_specs=(vm, vm),
        scratch_shapes=[
            pltpu.VMEM((2, groups, 3 * inner), bf),
            pltpu.VMEM((2, cols, width), bf),
            pltpu.SemaphoreType.DMA((2,)),
            pltpu.SemaphoreType.DMA((2,)),
            pltpu.SemaphoreType.DMA,
        ],
        compiler_params=pltpu.CompilerParams(vmem_limit_bytes=60 * MIB),
        cost_estimate=pl.CostEstimate(
            flops=2 * groups * cols * width * 3,
            bytes_accessed=3 * (groups + cols) * width * 2,
            transcendentals=0,
        ),
        name="first",
    )(sc, *args)


def latest(p, t):
    c = lax.axis_index("col")
    inside = jnp.logical_and(c > 0, c < lax.axis_size("col") - 1)
    return jnp.where(inside, p[...], t[...])


def mid_kernel(start, at, p, t, usel, acc, out):
    rows, width = out.shape[0], p.shape[1]
    lower = latest(p, t)
    for i in range(acc.shape[1] // TILE_N):
        c = slice(i * TILE_N, (i + 1) * TILE_N)
        out[:, c] = acc[start : start + rows, c] + lax.dot_general(
            lower, usel[c, at : at + width], NT, preferred_element_type=jnp.float32
        )


def mid(start, at, p, t, usel, acc):
    rows, width = p.shape
    cols = acc.shape[1]
    vm = pl.BlockSpec(memory_space=pltpu.VMEM)
    return pl.pallas_call(
        functools.partial(mid_kernel, start, at),
        out_shape=jax.ShapeDtypeStruct((rows, cols), acc.dtype),
        in_specs=[vm] * 4,
        out_specs=vm,
        compiler_params=pltpu.CompilerParams(vmem_limit_bytes=20 * MIB),
        cost_estimate=pl.CostEstimate(
            flops=2 * rows * cols * width, bytes_accessed=rows * cols * 8, transcendentals=0
        ),
    )(p, t, usel, acc)


def stage_kernel(x, acc, out):
    out[...] = x[...]


def stage(x, acc):
    vm = pl.BlockSpec(memory_space=pltpu.VMEM)
    return pl.pallas_call(
        stage_kernel,
        out_shape=jax.ShapeDtypeStruct(x.shape, x.dtype),
        in_specs=[vm, pl.BlockSpec(memory_space=pl.ANY)],
        out_specs=vm,
        compiler_params=pltpu.CompilerParams(vmem_limit_bytes=20 * MIB),
        cost_estimate=pl.CostEstimate(flops=0, bytes_accessed=4 * x.size, transcendentals=0),
        name="stage",
    )(x, acc)


def last_kernel(start, within, at, p, t, usel, acc, anc, piv, *rest):
    out, total, buf, sems = rest[-4:]
    rows, width = p.shape
    lanes = piv.shape[1]
    lower = latest(p, t)
    cols = acc.shape[1]
    per = cols // lanes
    for i in range(cols // TILE_N):
        c = slice(i * TILE_N, (i + 1) * TILE_N)
        total[:, c] = acc[within : within + rows, c] + lax.dot_general(
            lower, usel[c, at : at + width], NT, preferred_element_type=jnp.float32
        )
    some = rows // sems.shape[0]
    copies = []
    for g in range(sems.shape[0]):
        r = slice(g * some, (g + 1) * some)
        full = slice(start + g * some, start + (g + 1) * some)
        scale = piv[full, :]
        for h in range(per):
            k = slice(h * lanes, (h + 1) * lanes)
            buf[pl.ds(g * some * per + h, some, stride=per), :] = (
                anc[full, k].astype(jnp.float32) - total[r, k]
            ) * scale
        size = some * per
        copies.append(
            pltpu.make_async_copy(
                buf.at[pl.ds(g * size, size), :],
                out.at[pl.ds(start * per + g * size, size), :],
                sems.at[g],
            )
        )
        copies[-1].start()
    for copy in copies:
        copy.wait()


def last(start, within, at, p, t, usel, acc, anc, piv, before):
    groups, cols = anc.shape
    rows, width = p.shape
    lanes = piv.shape[1]
    vm = pl.BlockSpec(memory_space=pltpu.VMEM)
    in_specs = [vm] * 6
    args = [p, t, usel, acc, anc, piv]
    alias = {}
    if before is not None:
        in_specs.append(pl.BlockSpec(memory_space=pl.ANY))
        alias = {len(args): 0}
        args.append(before)
    return pl.pallas_call(
        functools.partial(last_kernel, start, within, at),
        out_shape=jax.ShapeDtypeStruct((groups * cols // lanes, lanes), jnp.float32),
        in_specs=in_specs,
        out_specs=pl.BlockSpec(memory_space=pl.ANY),
        scratch_shapes=[
            pltpu.VMEM((rows, cols), jnp.float32),
            pltpu.VMEM((rows * cols // lanes, lanes), jnp.float32),
            pltpu.SemaphoreType.DMA((1,)),
        ],
        input_output_aliases=alias,
        compiler_params=pltpu.CompilerParams(vmem_limit_bytes=20 * MIB),
        cost_estimate=pl.CostEstimate(
            flops=2 * rows * cols * width,
            bytes_accessed=cols * width * 2 + rows * width * 4 + rows * cols * 10,
            transcendentals=0,
        ),
    )(*args)


def two_layers(
    lower_panels, upper_panels, lower_lists, upper_lists, block_counts, ancestor, pivot_inverse
):
    r = lax.axis_index("row").astype(jnp.int32)
    c = lax.axis_index("col").astype(jnp.int32)
    _, rows, inner = lower_panels.shape
    cols = upper_panels.shape[1]
    groups = rows // 2
    count = block_counts.astype(jnp.int32)
    swap = [(0, 1), (1, 0)]
    outer = [(0, 1), (1, 0), (2, 3), (3, 2)]
    middle = [(1, 2), (2, 1)]
    ends = [(1, 0), (2, 3)]
    across = [(0, 2), (2, 0), (1, 3), (3, 1)]

    (lo,) = choose(head_kernel, lower_lists, lower_panels, [(groups, inner)], 1, 1, (10,), pltpu.VMEM)
    m0 = lax.ppermute(lo, "col", outer)
    n0 = lax.ppermute(lo, "col", middle)
    sizes = [(groups, inner), (groups, 2 * inner)]
    lk, ls = choose(lower_kernel, lower_lists, lower_panels, sizes, 2, 2, (5, 5))
    lrecv = lax.ppermute(ls, "layer", swap)
    sizes = [(cols, inner), (cols, inner // 2), (cols, inner // 2)]
    uo, uk, us = choose(upper_kernel, upper_lists, upper_panels, sizes, 0, 0, (1, 2))
    urecv = lax.ppermute(us, "layer", swap)
    bf = lo.dtype
    quarter = groups // 4
    part = [
        jax.ShapeDtypeStruct(((r1 - r0) * quarter, (c1 - c0) * inner), bf)
        for r0, r1, c0, c1 in PIECES
    ]
    lr = whole(lower_rest_kernel, part, count, lk, lrecv)
    half = [jax.ShapeDtypeStruct((cols // 2, inner + inner // 2), bf)] * 2
    up = whole(upper_rest_kernel, half, count, uo, uk, urecv)
    own = [lo, *lr]
    m = [m0] + [lax.ppermute(x, "col", outer) for x in lr]
    n = [n0] + [lax.ppermute(x, "col", middle) for x in lr]
    xx = [lax.ppermute(x, "row", outer) for x in up]
    yy = [lax.ppermute(x, "row", across) for x in up]
    da = lax.ppermute(yy[0], "row", outer)
    db = lax.ppermute(xx[1], "row", across)
    mine = [*up, *xx, *yy, da, db]
    mate = [lax.ppermute(x, "layer", swap) for x in mine]
    p = [lax.ppermute(x, "col", middle) for x in m]
    q = [lax.ppermute(x, "col", ends) for x in n]
    t = [lax.ppermute(x, "col", ends) for x in p]

    low = c < 2
    inside = jnp.logical_and(c > 0, c < 3)
    sc = jnp.stack(
        [
            r ^ c,
            r ^ c ^ 1,
            r ^ jnp.where(low, 2, 1),
            r ^ jnp.where(low, 3, 0),
            inside.astype(jnp.int32),
        ]
    ).astype(jnp.int32)
    acc, usel = first(sc, own, m, n, q, [*mine, *mate], groups, cols)
    anc = ancestor.reshape(groups, cols)
    piv = jnp.broadcast_to(pivot_inverse, (groups, LANES))
    acc = mid(0, 0, p[0], t[0], usel, acc)
    p[-1] = stage(p[-1], acc)
    out = None
    for (r0, _, c0, c1), x, y in zip(PIECES, p[1:], t[1:]):
        start, within, at = r0 * quarter, r0 * quarter, (1 + c0) * inner
        if c1 == 1:
            tail = mid(start, at, x, y, usel, acc)
            continue
        if c0 == 1:
            acc, within = tail, 0
        out = last(start, within, at, x, y, usel, acc, anc, piv, out)
    return out.reshape(groups, 1, cols)


def per_device(*args):
    sizes = [lax.axis_size(a) for a in ("layer", "row", "col")]
    if sizes == [2, 4, 4]:
        return two_layers(*args)
    return general(*args)


def solution(mesh):
    in_specs = (
        P("layer", "row", "col"),
        P("layer", "col", "row"),
        P("layer", None),
        P("layer", None),
        P("layer"),
        P("row", "layer", "col"),
        P("row", "layer"),
    )
    out_specs = P("row", "layer", "col")
    return jax.shard_map(
        per_device, mesh=mesh, in_specs=in_specs, out_specs=out_specs, check_vma=False
    )
```
